256 devices in a mesh: replica: 8 (over z_lo, x), fsdp: 32 (over z_hi, y, core).
Axes of the slice: x: 4, y: 4, z: 8 (z_hi: 4, z_lo: 2; z = z_hi * 2 + z_lo), core: 2. Of those that a mesh axis runs over, the one named last changes fastest.
Arguments:
- counts: int32 [8], P('replica'), may hold values from 100 to 1000
- inner: bfloat16 [8, 3, 2, 8192, 1024], P('replica', None, None, 'fsdp'), may hold values from -6 to 6
- anchor: bfloat16 [3, 2, 8192, 1024], P(None, None, 'fsdp'), may hold values from -6 to 6
- momentum: float32 [3, 2, 8192, 1024], P(None, None, ('fsdp', 'replica')), may hold values from -6 to 6
Outputs:
- new_weights: bfloat16 [3, 2, 8192, 1024], P(None, None, 'fsdp')
- new_momentum: float32 [3, 2, 8192, 1024], P(None, None, ('fsdp', 'replica'))
The draws below stay inside these ranges and needn't reach their ends.
Inputs may be any that keep to these rules, and one draw needn't show every extreme that they name: `counts`: inner steps of a group.
All inputs are finite; a program needn't handle non-finite values.
Results may differ from the reference program's by a relative error of at most 0.001.
Values may be sent and summed in bfloat16 or wider, within the bound.
A program may use at most 128 MiB of HBM per device.

```python
import jax
import jax.numpy as jnp

D = 8192
KVW = 1024
LAYERS = 3
GROUPS = 8


def place_ends(result, stream_key, low, high):
    index_at = [jax.random.randint(jax.random.fold_in(stream_key, axis), (), 0, length) for axis, length in enumerate(result.shape)]
    main_axis = result.shape.index(max(result.shape))
    neighbour = index_at[:main_axis] + [(index_at[main_axis] + 1) % result.shape[main_axis]] + index_at[main_axis + 1:]
    return result.at[tuple(index_at)].set(low).at[tuple(neighbour)].set(high)


def shard_levels(rng, dims, pieces, smallest, top_value):
    def one(dim, blocks):
        steps = jax.random.uniform(jax.random.fold_in(jax.random.fold_in(rng, 6), dim), (blocks,), jnp.float32, smallest / len(pieces), top_value / len(pieces))
        return jnp.repeat(jnp.exp(steps), dims[dim] // blocks).reshape((-1,) + (1,) * (len(dims) - dim - 1))

    loudness = one(*pieces[0])
    for cut in pieces[1:]:
        loudness = loudness * one(*cut)
    return loudness


def normal_values(stream_key, extent, deviation, limit, cuts=(), kind=jnp.bfloat16):
    entries = deviation * jax.random.normal(stream_key, extent, jnp.float32)
    if cuts:
        entries = entries * shard_levels(stream_key, extent, cuts, -0.22, 0.18)
    return jnp.clip(entries, -limit, limit).astype(kind)


def setup_inputs(seed: int = 0) -> dict:
    streams_of = jax.random.split(jax.random.key(seed), 5)
    counts = place_ends(jax.random.randint(streams_of[0], (GROUPS,), 100, 1001), jax.random.fold_in(streams_of[0], 1), 100, 1000).astype(jnp.int32)
    inner = normal_values(streams_of[1], (GROUPS, LAYERS, 2, D, KVW), 1.0, 6.0, ((0, 8), (3, 32)))
    anchor = normal_values(streams_of[2], (LAYERS, 2, D, KVW), 1.0, 6.0, ((2, 32),))
    momentum = normal_values(streams_of[3], (LAYERS, 2, D, KVW), 1.0, 6.0, ((2, 256),), jnp.float32)
    return {"counts": counts, "inner": inner, "anchor": anchor, "momentum": momentum}


outer_rate = 0.7
momentum_rate = 0.9


def reference(counts, inner, anchor, momentum):
    weights = counts.astype(jnp.float32)
    total = jnp.sum(weights)
    base = anchor.astype(jnp.float32)
    acc = jnp.zeros(anchor.shape, jnp.float32)
    for group in range(GROUPS):
        acc = acc + weights[group] * (base - inner[group].astype(jnp.float32))
    pseudo = acc / total
    new_momentum = momentum_rate * momentum + pseudo
    new_weights = (base - outer_rate * (pseudo + momentum_rate * new_momentum)).astype(jnp.bfloat16)
    return new_weights, new_momentum
```

```python
import functools

import jax
import jax.numpy as jnp
from jax import lax
from jax.experimental import pallas as pl
from jax.experimental.pallas import tpu as pltpu
from jax.sharding import PartitionSpec as P

MESH = pl.DeviceIdType.MESH

outer_rate = 0.7
momentum_rate = 0.9

RING = 4
ROWS = 2
ROWS_PER_CHUNK = 16
AHEAD = 2


def tiled(tile, shape):
    wide = jnp.concatenate([tile] * (shape[1] // tile.shape[1]), axis=1)
    return jnp.concatenate([wide] * (shape[0] // tile.shape[0]), axis=0)


def kernel(
    blocks, owned, width,
    counts, inner, anchor, momentum,
    weights_out, momentum_out,
    own, base, moment, got, count, part_sent, part_got, held, gathered, moment_next,
    load_sem, count_send, count_recv, store_sem, weight_sem,
    term_send, term_recv, part_send, part_recv, row_send, row_recv, col_send, col_recv,
):
    me = lax.axis_index("replica")
    row, column = me // RING, me % RING
    other = 1 - row
    across = other * RING + column
    beside = [row * RING + (column + d) % RING for d in range(1, RING)]
    per_block = owned // ROWS_PER_CHUNK
    chunks = blocks * per_block

    def place(c):
        return c // per_block, pl.ds((c % per_block) * ROWS_PER_CHUNK, ROWS_PER_CHUNK)

    def remote(src, dst, send, recv, device):
        return pltpu.make_async_remote_copy(
            src_ref=src,
            dst_ref=dst,
            send_sem=send,
            recv_sem=recv,
            device_id={"replica": device},
            device_id_type=MESH,
        )

    loads = [
        pltpu.make_async_copy(inner.at[:, :, column], own, load_sem.at[0]),
        pltpu.make_async_copy(anchor.at[:, :, column], base, load_sem.at[1]),
        pltpu.make_async_copy(momentum, moment, load_sem.at[2]),
    ]
    for load in loads:
        load.start()
    count[0] = jnp.full(count.shape[1:], counts[0].astype(jnp.float32))

    barrier = pltpu.get_barrier_semaphore()
    for device in [*beside, across]:
        pl.semaphore_signal(
            barrier, inc=1, device_id={"replica": device}, device_id_type=MESH
        )
    pl.semaphore_wait(barrier, RING)

    def count_copy(d):
        return remote(
            count.at[0], count.at[d], count_send.at[d], count_recv.at[d], beside[d - 1]
        )

    def row_count_copy():
        return remote(
            count.at[RING], count.at[RING + 1], count_send.at[0], count_recv.at[0], across
        )

    def term_copy(c, d):
        k, rows = place(c)
        return remote(
            inner.at[k, :, (column + d) % RING, rows],
            got.at[d - 1, k, :, rows],
            term_send.at[c, d - 1],
            term_recv.at[c, d - 1],
            beside[d - 1],
        )

    def part_copy(c):
        k, rows = place(c)
        return remote(
            part_sent.at[k, rows],
            part_got.at[k, rows],
            part_send.at[c],
            part_recv.at[c],
            across,
        )

    def row_copy(c, d):
        k, rows = place(c)
        mine = gathered.at[k, row, column, rows]
        return remote(mine, mine, row_send.at[c, d - 1], row_recv.at[c, d - 1], beside[d - 1])

    def col_copy(c, d):
        k, rows = place(c)
        slab = gathered.at[k, row, (column + RING - d) % RING, rows]
        return remote(slab, slab, col_send.at[c, d], col_recv.at[c, d], across)

    def moment_store(c):
        k, rows = place(c)
        return pltpu.make_async_copy(
            moment_next.at[k, rows], momentum_out.at[k, rows], store_sem.at[c]
        )

    def weight_store(c):
        k, rows = place(c)
        return pltpu.make_async_copy(
            gathered.at[k, :, :, rows], weights_out.at[k, :, :, rows], weight_sem.at[c]
        )

    shape = (ROWS_PER_CHUNK, width)

    def weighted(c, r):
        k, rows = place(c)
        start = base[k, r, rows].astype(jnp.float32)
        total = tiled(count[0], shape) * (start - own[k, r, rows].astype(jnp.float32))
        for d in range(1, RING):
            total = total + tiled(count[d], shape) * (
                start - got[d - 1, k, r, rows].astype(jnp.float32)
            )
        return start, total

    def send_terms(c):
        for d in range(1, RING):
            term_copy(c, d).start()

    def send_part(c):
        for d in range(1, RING):
            term_copy(c, d).wait_recv()
        k, rows = place(c)
        part_sent[k, rows] = weighted(c, other)[1]
        part_copy(c).start()
        held[k, rows] = weighted(c, row)[1]

    def update(c):
        part_copy(c).wait_recv()
        k, rows = place(c)
        start = base[k, row, rows].astype(jnp.float32)
        pseudo = (held[k, rows] + part_got[k, rows]) * tiled(count[RING + 2], shape)
        next_moment = momentum_rate * moment[k, rows] + pseudo
        next_weights = start - outer_rate * (pseudo + momentum_rate * next_moment)
        gathered[k, row, column, rows] = next_weights.astype(gathered.dtype)
        moment_next[k, rows] = next_moment
        for d in range(1, RING):
            row_copy(c, d).start()
        col_copy(c, 0).start()
        moment_store(c).start()

    def forward(c):
        for d in range(1, RING):
            row_copy(c, d).wait_recv()
            col_copy(c, d).start()

    def finish(c):
        for d in range(RING):
            col_copy(c, d).wait_recv()
        weight_store(c).start()

    for d in range(1, RING):
        count_copy(d).start()
    for c in range(min(AHEAD, chunks)):
        send_terms(c)
    for d in range(1, RING):
        count_copy(d).wait_recv()
    count[RING] = count[0] + count[1] + count[2] + count[3]
    row_count_copy().start()
    for load in loads:
        load.wait()

    for t in range(chunks + 4):
        if t < chunks:
            send_part(t)
        if t == 0:
            row_count_copy().wait_recv()
            count[RING + 2] = 1.0 / (count[RING] + count[RING + 1])
        if t + AHEAD < chunks:
            send_terms(t + AHEAD)
        if 0 <= t - 1 < chunks:
            update(t - 1)
        if 0 <= t - 2 < chunks:
            forward(t - 2)
        if 0 <= t - 4 < chunks:
            finish(t - 4)

    for d in range(1, RING):
        count_copy(d).wait_send()
    row_count_copy().wait_send()
    for c in range(chunks):
        for d in range(1, RING):
            term_copy(c, d).wait_send()
            row_copy(c, d).wait_send()
        part_copy(c).wait_send()
        for d in range(RING):
            col_copy(c, d).wait_send()
        moment_store(c).wait()
        weight_store(c).wait()


def on_device(counts, inner, anchor, momentum):
    layers, kinds, owned, width = momentum.shape
    blocks = layers * kinds
    chunks = blocks * (owned // ROWS_PER_CHUNK)
    split = (blocks, ROWS, RING, owned, width)
    dma = pltpu.SemaphoreType.DMA
    anywhere = pl.BlockSpec(memory_space=pl.ANY)
    weights, moments = pl.pallas_call(
        functools.partial(kernel, blocks, owned, width),
        out_shape=(
            jax.ShapeDtypeStruct(split, anchor.dtype),
            jax.ShapeDtypeStruct((blocks, owned, width), momentum.dtype),
        ),
        in_specs=[pl.BlockSpec(memory_space=pltpu.SMEM), anywhere, anywhere, anywhere],
        out_specs=(anywhere, anywhere),
        scratch_shapes=[
            pltpu.VMEM((blocks, ROWS, owned, width), inner.dtype),
            pltpu.VMEM((blocks, ROWS, owned, width), anchor.dtype),
            pltpu.VMEM((blocks, owned, width), jnp.float32),
            pltpu.VMEM((RING - 1, blocks, ROWS, owned, width), inner.dtype),
            pltpu.VMEM((RING + 3, 8, 128), jnp.float32),
            pltpu.VMEM((blocks, owned, width), jnp.float32),
            pltpu.VMEM((blocks, owned, width), jnp.float32),
            pltpu.VMEM((blocks, owned, width), jnp.float32),
            pltpu.VMEM(split, anchor.dtype),
            pltpu.VMEM((blocks, owned, width), jnp.float32),
            dma((3,)),
            dma((RING,)),
            dma((RING,)),
            dma((chunks,)),
            dma((chunks,)),
            dma((chunks, RING - 1)),
            dma((chunks, RING - 1)),
            dma((chunks,)),
            dma((chunks,)),
            dma((chunks, RING - 1)),
            dma((chunks, RING - 1)),
            dma((chunks, RING)),
            dma((chunks, RING)),
        ],
        compiler_params=pltpu.CompilerParams(
            collective_id=0, has_side_effects=True, vmem_limit_bytes=40 << 20
        ),
        name="outer_step",
    )(
        counts,
        inner.reshape(split),
        anchor.reshape(split),
        momentum.reshape(blocks, owned, width),
    )
    return weights.reshape(anchor.shape), moments.reshape(momentum.shape)


def solution(mesh):
    placed = (
        P("replica"),
        P("replica", None, None, "fsdp", None),
        P(None, None, "fsdp", None),
        P(None, None, ("fsdp", "replica"), None),
    )
    return jax.shard_map(
        on_device,
        mesh=mesh,
        in_specs=placed,
        out_specs=(P(None, None, "fsdp", None), P(None, None, ("fsdp", "replica"), None)),
        check_vma=False,
    )
```

```python
import functools

import jax
import jax.numpy as jnp
from jax import lax
from jax.experimental import pallas as pl
from jax.experimental.pallas import tpu as pltpu
from jax.sharding import PartitionSpec as P

MESH = pl.DeviceIdType.MESH

outer_rate = 0.7
momentum_rate = 0.9

RING = 4
ROWS = 2
GROUP = 16
PARTS = (1,) * 12
AHEAD = 24.0
UPDATE_LAG = 32.0
RELAY_LAG = 48.0
FORWARD_LAG = 64.0
FINISH_LAG = 96.0
ORDER = "purxfs"
LATE = 96
TURNED = (1, 3)
NEXT = (1, 3)


def chunk_list(blocks, owned, width):
    chunks, done = [], 0.0
    for group in range(blocks * owned // GROUP):
        k, row = divmod(group * GROUP, owned)
        cols = width // PARTS[group]
        for col in range(0, width, cols):
            after = done + GROUP * cols / width
            chunks.append((k, row, GROUP, col, cols, done, after))
            done = after
    return chunks


def schedule(chunks):
    steps = []
    for c, (*_, before, after) in enumerate(chunks):
        steps += [
            (max(before - AHEAD, 0.0), ORDER.index("s"), c, "s"),
            (after, ORDER.index("p"), c, "p"),
            (after + UPDATE_LAG, ORDER.index("u"), c, "u"),
            (after + FORWARD_LAG, ORDER.index("f"), c, "f"),
            (after + RELAY_LAG, ORDER.index("r"), c, "r"),
            (after + RELAY_LAG, ORDER.index("x"), c, "x"),
            (after + FINISH_LAG, len(ORDER), c, "e"),
        ]
    return [(stage, c) for _, _, c, stage in sorted(steps)]


def tiled(tile, shape):
    wide = jnp.concatenate([tile] * (shape[1] // tile.shape[1]), axis=1)
    return jnp.concatenate([wide] * (shape[0] // tile.shape[0]), axis=0)


def kernel(
    blocks, owned, width,
    counts, inner, anchor, momentum,
    gathered, moment_next,
    own, base, moment, got, count, part_sent, part_got, held,
    load_sem, count_send, count_recv,
    term_send, term_recv, part_send, part_recv, row_send, row_recv, col_send, col_recv,
):
    me = lax.axis_index("replica")
    row, column = me // RING, me % RING
    other = 1 - row
    across = other * RING + column
    beside = [row * RING + (column + d) % RING for d in range(1, RING)]
    pieces = chunk_list(blocks, owned, width)
    chunks = len(pieces)

    def place(c):
        k, row, rows, col, cols, _, _ = pieces[c]
        return k, pl.ds(row, rows), pl.ds(col, cols)

    def along_x(c):
        return TURNED if pieces[c][5] >= blocks * owned - LATE else ()

    def remote(src, dst, send, recv, device):
        return pltpu.make_async_remote_copy(
            src_ref=src,
            dst_ref=dst,
            send_sem=send,
            recv_sem=recv,
            device_id={"replica": device},
            device_id_type=MESH,
        )

    loads = [
        pltpu.make_async_copy(inner.at[:, :, column], own, load_sem.at[0]),
        pltpu.make_async_copy(anchor.at[:, :, column], base, load_sem.at[1]),
        pltpu.make_async_copy(momentum, moment, load_sem.at[2]),
    ]
    for load in loads:
        load.start()
    count[0] = jnp.full(count.shape[1:], counts[0].astype(jnp.float32))

    barrier = pltpu.get_barrier_semaphore()
    for device in [*beside, across]:
        pl.semaphore_signal(
            barrier, inc=1, device_id={"replica": device}, device_id_type=MESH
        )
    pl.semaphore_wait(barrier, RING)

    def count_copy(d):
        return remote(
            count.at[0], count.at[d], count_send.at[d], count_recv.at[d], beside[d - 1]
        )

    def row_count_copy():
        return remote(
            count.at[RING], count.at[RING + 1], count_send.at[0], count_recv.at[0], across
        )

    def term_copy(c, d):
        k, rows, cols = place(c)
        return remote(
            inner.at[k, :, (column + d) % RING, rows, cols],
            got.at[d - 1, k, :, rows, cols],
            term_send.at[c, d - 1],
            term_recv.at[c, d - 1],
            beside[d - 1],
        )

    def part_copy(c):
        k, rows, cols = place(c)
        return remote(
            part_sent.at[k, rows, cols],
            part_got.at[k, rows, cols],
            part_send.at[c],
            part_recv.at[c],
            across,
        )

    def row_copy(c, d):
        k, rows, cols = place(c)
        mine = gathered.at[k, row, column, rows, cols]
        return remote(mine, mine, row_send.at[c, d], row_recv.at[c, d], beside[d - 1])

    def relay_copy(c, d):
        k, rows, _ = place(c)
        half = pieces[c][4] // 2
        cols = pl.ds(pieces[c][3] + (0 if d == 1 else half), half)
        slab = gathered.at[k, row, (column + RING - d) % RING, rows, cols]
        return remote(
            slab, slab, row_send.at[c, d - 1], row_recv.at[c, d - 1], beside[d - 1]
        )

    def col_copy(c, d):
        k, rows, cols = place(c)
        slab = gathered.at[k, row, (column + RING - d) % RING, rows, cols]
        return remote(slab, slab, col_send.at[c, d], col_recv.at[c, d], across)

    def turn_copy(c, d):
        k, rows, cols = place(c)
        slab = gathered.at[k, other, column, rows, cols]
        return remote(slab, slab, col_send.at[c, d], col_recv.at[c, d], beside[d - 1])

    def shape(c):
        return pieces[c][2], pieces[c][4]

    def weighted(c, r):
        k, rows, cols = place(c)
        start = base[k, r, rows, cols].astype(jnp.float32)
        total = tiled(count[0], shape(c)) * (start - own[k, r, rows, cols].astype(jnp.float32))
        for d in range(1, RING):
            total = total + tiled(count[d], shape(c)) * (
                start - got[d - 1, k, r, rows, cols].astype(jnp.float32)
            )
        return start, total

    def send_terms(c):
        for d in range(1, RING):
            term_copy(c, d).start()

    def send_part(c):
        for d in range(1, RING):
            term_copy(c, d).wait_recv()
        k, rows, cols = place(c)
        part_sent[k, rows, cols] = weighted(c, other)[1]
        part_copy(c).start()
        held[k, rows, cols] = weighted(c, row)[1]

    def update(c):
        part_copy(c).wait_recv()
        k, rows, cols = place(c)
        start = base[k, row, rows, cols].astype(jnp.float32)
        pseudo = (held[k, rows, cols] + part_got[k, rows, cols]) * tiled(count[RING + 2], shape(c))
        next_moment = momentum_rate * moment[k, rows, cols] + pseudo
        next_weights = start - outer_rate * (pseudo + momentum_rate * next_moment)
        gathered[k, row, column, rows, cols] = next_weights.astype(gathered.dtype)
        moment_next[k, rows, cols] = next_moment
        for d in NEXT:
            row_copy(c, d).start()
        col_copy(c, 0).start()

    def relay(c):
        for d in NEXT:
            row_copy(c, d).wait_recv()
            relay_copy(c, d).start()
            if d not in along_x(c):
                col_copy(c, d).start()

    def forward(c):
        for d in NEXT:
            relay_copy(c, d).wait_recv()
        col_copy(c, 2).start()

    def turn(c):
        col_copy(c, 0).wait_recv()
        for d in along_x(c):
            turn_copy(c, d).start()

    def finish(c):
        for d in range(1, RING):
            col_copy(c, d).wait_recv()

    for d in range(1, RING):
        count_copy(d).start()
    steps = schedule(pieces)
    first = steps.index(("p", 0))
    for stage, c in steps[:first]:
        send_terms(c)
    for d in range(1, RING):
        count_copy(d).wait_recv()
    count[RING] = count[0] + count[1] + count[2] + count[3]
    row_count_copy().start()
    for load in loads:
        load.wait()

    run = {"r": relay, "s": send_terms, "p": send_part, "u": update, "f": forward, "x": turn, "e": finish}
    for stage, c in steps[first:]:
        if stage == "u" and c == 0:
            row_count_copy().wait_recv()
            count[RING + 2] = 1.0 / (count[RING] + count[RING + 1])
        run[stage](c)

    for d in range(1, RING):
        count_copy(d).wait_send()
    row_count_copy().wait_send()
    for c in range(chunks):
        for d in range(1, RING):
            term_copy(c, d).wait_send()
        for d in NEXT:
            row_copy(c, d).wait_send()
            relay_copy(c, d).wait_send()
        part_copy(c).wait_send()
        for d in range(RING):
            col_copy(c, d).wait_send()


def store_kernel(weights, moments, weights_out, moments_out, sem):
    copies = [
        pltpu.make_async_copy(weights, weights_out, sem.at[0]),
        pltpu.make_async_copy(moments, moments_out, sem.at[1]),
    ]
    for copy in copies:
        copy.start()
    for copy in copies:
        copy.wait()


def store(weights, moments):
    anywhere = pl.BlockSpec(memory_space=pl.ANY)
    return pl.pallas_call(
        store_kernel,
        out_shape=(
            jax.ShapeDtypeStruct(weights.shape, weights.dtype),
            jax.ShapeDtypeStruct(moments.shape, moments.dtype),
        ),
        in_specs=[anywhere, anywhere],
        out_specs=(anywhere, anywhere),
        scratch_shapes=[pltpu.SemaphoreType.DMA((2,))],
        compiler_params=pltpu.CompilerParams(vmem_limit_bytes=4 << 20),
        name="store",
    )(weights, moments)


def on_device(counts, inner, anchor, momentum):
    layers, kinds, owned, width = momentum.shape
    blocks = layers * kinds
    chunks = len(chunk_list(blocks, owned, width))
    split = (blocks, ROWS, RING, owned, width)
    dma = pltpu.SemaphoreType.DMA
    anywhere = pl.BlockSpec(memory_space=pltpu.HBM)
    weights, moments = pl.pallas_call(
        functools.partial(kernel, blocks, owned, width),
        out_shape=(
            jax.ShapeDtypeStruct(split, anchor.dtype),
            jax.ShapeDtypeStruct((blocks, owned, width), momentum.dtype),
        ),
        in_specs=[pl.BlockSpec(memory_space=pltpu.SMEM), anywhere, anywhere, anywhere],
        out_specs=(pl.BlockSpec(memory_space=pltpu.VMEM),) * 2,
        scratch_shapes=[
            pltpu.VMEM((blocks, ROWS, owned, width), inner.dtype),
            pltpu.VMEM((blocks, ROWS, owned, width), anchor.dtype),
            pltpu.VMEM((blocks, owned, width), jnp.float32),
            pltpu.VMEM((RING - 1, blocks, ROWS, owned, width), inner.dtype),
            pltpu.VMEM((RING + 3, 8, 128), jnp.float32),
            pltpu.VMEM((blocks, owned, width), jnp.float32),
            pltpu.VMEM((blocks, owned, width), jnp.float32),
            pltpu.VMEM((blocks, owned, width), jnp.float32),
            dma((3,)),
            dma((RING,)),
            dma((RING,)),
            dma((chunks, RING - 1)),
            dma((chunks, RING - 1)),
            dma((chunks,)),
            dma((chunks,)),
            dma((chunks, RING)),
            dma((chunks, RING)),
            dma((chunks, RING)),
            dma((chunks, RING)),
        ],
        compiler_params=pltpu.CompilerParams(
            collective_id=0, has_side_effects=True, vmem_limit_bytes=40 << 20
        ),
        name="outer_step",
    )(
        counts,
        pltpu.with_memory_space_constraint(inner.reshape(split), pltpu.HBM),
        pltpu.with_memory_space_constraint(anchor.reshape(split), pltpu.HBM),
        pltpu.with_memory_space_constraint(momentum.reshape(blocks, owned, width), pltpu.HBM),
    )
    weights, moments = store(weights, moments)
    return weights.reshape(anchor.shape), moments.reshape(momentum.shape)


def solution(mesh):
    placed = (
        P("replica"),
        P("replica", None, None, "fsdp", None),
        P(None, None, "fsdp", None),
        P(None, None, ("fsdp", "replica"), None),
    )
    return jax.shard_map(
        on_device,
        mesh=mesh,
        in_specs=placed,
        out_specs=(P(None, None, "fsdp", None), P(None, None, ("fsdp", "replica"), None)),
        check_vma=False,
    )
```

```python
import functools

import jax
import jax.numpy as jnp
from jax import lax
from jax.experimental import pallas as pl
from jax.experimental.pallas import tpu as pltpu
from jax.sharding import PartitionSpec as P

MESH = pl.DeviceIdType.MESH

outer_rate = 0.7
momentum_rate = 0.9

RING = 4
ROWS = 2
SIZES = (16,) * 12
AHEAD = 32.0
UPDATE_LAG = 24.0
RELAY_LAG = 56.0
FORWARD_LAG = 88.0
FINISH_LAG = 120.0
ORDER = "purxfs"
LATE = 96
TURNED = (1, 3)
NEXT = (1, 3)


def chunk_list(owned, width):
    chunks, done = [], 0
    for rows in SIZES:
        k, row = divmod(done, owned)
        chunks.append((k, row, rows, 0, width, done, done + rows))
        done += rows
    return chunks


def schedule(chunks):
    steps = []
    for c, (*_, before, after) in enumerate(chunks):
        steps += [
            (max(before - AHEAD, 0.0), ORDER.index("s"), c, "s"),
            (after, ORDER.index("p"), c, "p"),
            (after + UPDATE_LAG, ORDER.index("u"), c, "u"),
            (after + FORWARD_LAG, ORDER.index("f"), c, "f"),
            (after + RELAY_LAG, ORDER.index("r"), c, "r"),
            (after + RELAY_LAG, ORDER.index("x"), c, "x"),
            (after + FINISH_LAG, len(ORDER), c, "e"),
        ]
    return [(stage, c) for _, _, c, stage in sorted(steps)]


def tiled(tile, shape):
    wide = jnp.concatenate([tile] * (shape[1] // tile.shape[1]), axis=1)
    return jnp.concatenate([wide] * (shape[0] // tile.shape[0]), axis=0)


def kernel(
    blocks, owned, width,
    counts, inner, anchor, momentum,
    gathered, moment_next,
    own, base, moment, got, count, part_sent, part_got, held,
    load_sem, count_send, count_recv,
    term_send, term_recv, part_send, part_recv, row_send, row_recv, col_send, col_recv,
):
    me = lax.axis_index("replica")
    row, column = me // RING, me % RING
    other = 1 - row
    across = other * RING + column
    beside = [row * RING + (column + d) % RING for d in range(1, RING)]
    pieces = chunk_list(owned, width)
    chunks = len(pieces)

    def place(c):
        k, row, rows, col, cols, _, _ = pieces[c]
        return k, pl.ds(row, rows), pl.ds(col, cols)

    def along_x(c):
        return TURNED if pieces[c][5] >= blocks * owned - LATE else ()

    def remote(src, dst, send, recv, device):
        return pltpu.make_async_remote_copy(
            src_ref=src,
            dst_ref=dst,
            send_sem=send,
            recv_sem=recv,
            device_id={"replica": device},
            device_id_type=MESH,
        )

    loads = [
        pltpu.make_async_copy(inner.at[:, :, column], own, load_sem.at[0]),
        pltpu.make_async_copy(anchor.at[:, :, column], base, load_sem.at[1]),
        pltpu.make_async_copy(momentum, moment, load_sem.at[2]),
    ]
    for load in loads:
        load.start()
    count[0] = jnp.full(count.shape[1:], counts[0].astype(jnp.float32))

    barrier = pltpu.get_barrier_semaphore()
    for device in [*beside, across]:
        pl.semaphore_signal(
            barrier, inc=1, device_id={"replica": device}, device_id_type=MESH
        )
    pl.semaphore_wait(barrier, RING)

    def count_copy(d):
        return remote(
            count.at[0], count.at[d], count_send.at[d], count_recv.at[d], beside[d - 1]
        )

    def row_count_copy():
        return remote(
            count.at[RING], count.at[RING + 1], count_send.at[0], count_recv.at[0], across
        )

    def term_copy(c, d):
        k, rows, cols = place(c)
        return remote(
            inner.at[k, :, (column + d) % RING, rows, cols],
            got.at[d - 1, k, :, rows, cols],
            term_send.at[c, d - 1],
            term_recv.at[c, d - 1],
            beside[d - 1],
        )

    def part_copy(c):
        k, rows, cols = place(c)
        return remote(
            part_sent.at[k, rows, cols],
            part_got.at[k, rows, cols],
            part_send.at[c],
            part_recv.at[c],
            across,
        )

    def row_copy(c, d):
        k, rows, cols = place(c)
        mine = gathered.at[k, row, column, rows, cols]
        return remote(mine, mine, row_send.at[c, d], row_recv.at[c, d], beside[d - 1])

    def relay_copy(c, d):
        k, rows, _ = place(c)
        half = pieces[c][4] // 2
        cols = pl.ds(pieces[c][3] + (0 if d == 1 else half), half)
        slab = gathered.at[k, row, (column + RING - d) % RING, rows, cols]
        return remote(
            slab, slab, row_send.at[c, d - 1], row_recv.at[c, d - 1], beside[d - 1]
        )

    def col_copy(c, d):
        k, rows, cols = place(c)
        slab = gathered.at[k, row, (column + RING - d) % RING, rows, cols]
        return remote(slab, slab, col_send.at[c, d], col_recv.at[c, d], across)

    def turn_copy(c, d):
        k, rows, cols = place(c)
        slab = gathered.at[k, other, column, rows, cols]
        return remote(slab, slab, col_send.at[c, d], col_recv.at[c, d], beside[d - 1])

    def shape(c):
        return pieces[c][2], pieces[c][4]

    def weighted(c, r):
        k, rows, cols = place(c)
        start = base[k, r, rows, cols].astype(jnp.float32)
        total = tiled(count[0], shape(c)) * (start - own[k, r, rows, cols].astype(jnp.float32))
        for d in range(1, RING):
            total = total + tiled(count[d], shape(c)) * (
                start - got[d - 1, k, r, rows, cols].astype(jnp.float32)
            )
        return start, total

    def send_terms(c):
        for d in range(1, RING):
            term_copy(c, d).start()

    def send_part(c):
        for d in range(1, RING):
            term_copy(c, d).wait_recv()
        k, rows, cols = place(c)
        part_sent[k, rows, cols] = weighted(c, other)[1]
        part_copy(c).start()
        held[k, rows, cols] = weighted(c, row)[1]

    def update(c):
        part_copy(c).wait_recv()
        k, rows, cols = place(c)
        start = base[k, row, rows, cols].astype(jnp.float32)
        pseudo = (held[k, rows, cols] + part_got[k, rows, cols]) * tiled(count[RING + 2], shape(c))
        next_moment = momentum_rate * moment[k, rows, cols] + pseudo
        next_weights = start - outer_rate * (pseudo + momentum_rate * next_moment)
        gathered[k, row, column, rows, cols] = next_weights.astype(gathered.dtype)
        moment_next[k, rows, cols] = next_moment
        for d in NEXT:
            row_copy(c, d).start()
        col_copy(c, 0).start()

    def relay(c):
        for d in NEXT:
            row_copy(c, d).wait_recv()
            relay_copy(c, d).start()
            if d not in along_x(c):
                col_copy(c, d).start()

    def forward(c):
        for d in NEXT:
            relay_copy(c, d).wait_recv()
        col_copy(c, 2).start()

    def turn(c):
        col_copy(c, 0).wait_recv()
        for d in along_x(c):
            turn_copy(c, d).start()

    def finish(c):
        for d in range(1, RING):
            col_copy(c, d).wait_recv()

    for d in range(1, RING):
        count_copy(d).start()
    steps = schedule(pieces)
    first = steps.index(("p", 0))
    for stage, c in steps[:first]:
        send_terms(c)
    for d in range(1, RING):
        count_copy(d).wait_recv()
    count[RING] = count[0] + count[1] + count[2] + count[3]
    row_count_copy().start()
    for load in loads:
        load.wait()

    run = {"r": relay, "s": send_terms, "p": send_part, "u": update, "f": forward, "x": turn, "e": finish}
    for stage, c in steps[first:]:
        if stage == "u" and c == 0:
            row_count_copy().wait_recv()
            count[RING + 2] = 1.0 / (count[RING] + count[RING + 1])
        run[stage](c)

    for d in range(1, RING):
        count_copy(d).wait_send()
    row_count_copy().wait_send()
    for c in range(chunks):
        for d in range(1, RING):
            term_copy(c, d).wait_send()
        for d in NEXT:
            row_copy(c, d).wait_send()
            relay_copy(c, d).wait_send()
        part_copy(c).wait_send()
        for d in range(RING):
            col_copy(c, d).wait_send()


def store_kernel(weights, moments, weights_out, moments_out, sem):
    copies = [
        pltpu.make_async_copy(weights, weights_out, sem.at[0]),
        pltpu.make_async_copy(moments, moments_out, sem.at[1]),
    ]
    for copy in copies:
        copy.start()
    for copy in copies:
        copy.wait()


def store(weights, moments):
    anywhere = pl.BlockSpec(memory_space=pl.ANY)
    return pl.pallas_call(
        store_kernel,
        out_shape=(
            jax.ShapeDtypeStruct(weights.shape, weights.dtype),
            jax.ShapeDtypeStruct(moments.shape, moments.dtype),
        ),
        in_specs=[anywhere, anywhere],
        out_specs=(anywhere, anywhere),
        scratch_shapes=[pltpu.SemaphoreType.DMA((2,))],
        compiler_params=pltpu.CompilerParams(vmem_limit_bytes=4 << 20),
        name="store",
    )(weights, moments)


def on_device(counts, inner, anchor, momentum):
    layers, kinds, owned, width = momentum.shape
    blocks = layers * kinds
    chunks = len(chunk_list(owned, width))
    split = (blocks, ROWS, RING, owned, width)
    dma = pltpu.SemaphoreType.DMA
    anywhere = pl.BlockSpec(memory_space=pltpu.HBM)
    weights, moments = pl.pallas_call(
        functools.partial(kernel, blocks, owned, width),
        out_shape=(
            jax.ShapeDtypeStruct(split, anchor.dtype),
            jax.ShapeDtypeStruct((blocks, owned, width), momentum.dtype),
        ),
        in_specs=[pl.BlockSpec(memory_space=pltpu.SMEM), anywhere, anywhere, anywhere],
        out_specs=(pl.BlockSpec(memory_space=pltpu.VMEM),) * 2,
        scratch_shapes=[
            pltpu.VMEM((blocks, ROWS, owned, width), inner.dtype),
            pltpu.VMEM((blocks, ROWS, owned, width), anchor.dtype),
            pltpu.VMEM((blocks, owned, width), jnp.float32),
            pltpu.VMEM((RING - 1, blocks, ROWS, owned, width), inner.dtype),
            pltpu.VMEM((RING + 3, 8, 128), jnp.float32),
            pltpu.VMEM((blocks, owned, width), jnp.float32),
            pltpu.VMEM((blocks, owned, width), jnp.float32),
            pltpu.VMEM((blocks, owned, width), jnp.float32),
            dma((3,)),
            dma((RING,)),
            dma((RING,)),
            dma((chunks, RING - 1)),
            dma((chunks, RING - 1)),
            dma((chunks,)),
            dma((chunks,)),
            dma((chunks, RING)),
            dma((chunks, RING)),
            dma((chunks, RING)),
            dma((chunks, RING)),
        ],
        compiler_params=pltpu.CompilerParams(
            collective_id=0, has_side_effects=True, vmem_limit_bytes=40 << 20
        ),
        name="outer_step",
    )(
        counts,
        pltpu.with_memory_space_constraint(inner.reshape(split), pltpu.HBM),
        pltpu.with_memory_space_constraint(anchor.reshape(split), pltpu.HBM),
        pltpu.with_memory_space_constraint(momentum.reshape(blocks, owned, width), pltpu.HBM),
    )
    weights, moments = store(weights, moments)
    return weights.reshape(anchor.shape), moments.reshape(momentum.shape)


def solution(mesh):
    placed = (
        P("replica"),
        P("replica", None, None, "fsdp", None),
        P(None, None, "fsdp", None),
        P(None, None, ("fsdp", "replica"), None),
    )
    return jax.shard_map(
        on_device,
        mesh=mesh,
        in_specs=placed,
        out_specs=(P(None, None, "fsdp", None), P(None, None, ("fsdp", "replica"), None)),
        check_vma=False,
    )
```

```python
import functools

import jax
import jax.numpy as jnp
from jax import lax
from jax.experimental import pallas as pl
from jax.experimental.pallas import tpu as pltpu
from jax.sharding import PartitionSpec as P

MESH = pl.DeviceIdType.MESH

outer_rate = 0.7
momentum_rate = 0.9

RING = 4
ROWS = 2
SIZES = (16,) * 12
AHEAD = 32.0
UPDATE_LAG = 24.0
RELAY_LAG = 56.0
TURN_LAG = 72.0
FORWARD_LAG = 88.0
FINISH_LAG = 1000.0
ORDER = "purxfs"
LATE = 96
TURNED = (1, 3)
NEXT = (1, 3)


def chunk_list(owned, width):
    chunks, done = [], 0
    for rows in SIZES:
        k, row = divmod(done, owned)
        chunks.append((k, row, rows, 0, width, done, done + rows))
        done += rows
    return chunks


def schedule(chunks):
    steps = []
    for c, (*_, before, after) in enumerate(chunks):
        steps += [
            (max(before - AHEAD, 0.0), ORDER.index("s"), c, "s"),
            (after, ORDER.index("p"), c, "p"),
            (after + UPDATE_LAG, ORDER.index("u"), c, "u"),
            (after + FORWARD_LAG, ORDER.index("f"), c, "f"),
            (after + RELAY_LAG, ORDER.index("r"), c, "r"),
            (after + TURN_LAG, ORDER.index("x"), c, "x"),
            (after + FINISH_LAG, len(ORDER), c, "e"),
        ]
    return [(stage, c) for _, _, c, stage in sorted(steps)]


def tiled(tile, shape):
    wide = jnp.concatenate([tile] * (shape[1] // tile.shape[1]), axis=1)
    return jnp.concatenate([wide] * (shape[0] // tile.shape[0]), axis=0)


def kernel(
    blocks, owned, width,
    counts, inner, anchor, momentum,
    gathered, moment_next,
    own, base, moment, got, count, part_sent, part_got, held,
    load_sem, count_send, count_recv,
    term_send, term_recv, part_send, part_recv, row_send, row_recv, col_send, col_recv,
):
    me = lax.axis_index("replica")
    row, column = me // RING, me % RING
    other = 1 - row
    across = other * RING + column
    beside = [row * RING + (column + d) % RING for d in range(1, RING)]
    pieces = chunk_list(owned, width)
    chunks = len(pieces)

    def place(c):
        k, row, rows, col, cols, _, _ = pieces[c]
        return k, pl.ds(row, rows), pl.ds(col, cols)

    def along_x(c):
        return TURNED if pieces[c][5] >= blocks * owned - LATE else ()

    def remote(src, dst, send, recv, device):
        return pltpu.make_async_remote_copy(
            src_ref=src,
            dst_ref=dst,
            send_sem=send,
            recv_sem=recv,
            device_id={"replica": device},
            device_id_type=MESH,
        )

    barrier = pltpu.get_barrier_semaphore()
    for device in [*beside, across]:
        pl.semaphore_signal(
            barrier, inc=1, device_id={"replica": device}, device_id_type=MESH
        )
    loads = [
        pltpu.make_async_copy(inner.at[:, :, column], own, load_sem.at[0]),
        pltpu.make_async_copy(anchor.at[:, :, column], base, load_sem.at[1]),
        pltpu.make_async_copy(momentum, moment, load_sem.at[2]),
    ]
    for load in loads:
        load.start()
    count[0] = jnp.full(count.shape[1:], counts[0].astype(jnp.float32))

    pl.semaphore_wait(barrier, RING)

    def count_copy(d):
        return remote(
            count.at[0], count.at[d], count_send.at[d], count_recv.at[d], beside[d - 1]
        )

    def row_count_copy():
        return remote(
            count.at[RING], count.at[RING + 1], count_send.at[0], count_recv.at[0], across
        )

    def term_copy(c, d):
        k, rows, cols = place(c)
        return remote(
            inner.at[k, :, (column + d) % RING, rows, cols],
            got.at[d - 1, k, :, rows, cols],
            term_send.at[c, d - 1],
            term_recv.at[c, d - 1],
            beside[d - 1],
        )

    def part_copy(c):
        k, rows, cols = place(c)
        return remote(
            part_sent.at[k, rows, cols],
            part_got.at[k, rows, cols],
            part_send.at[c],
            part_recv.at[c],
            across,
        )

    def row_copy(c, d):
        k, rows, cols = place(c)
        mine = gathered.at[k, row, column, rows, cols]
        return remote(mine, mine, row_send.at[c, d], row_recv.at[c, d], beside[d - 1])

    def relay_copy(c, d):
        k, rows, _ = place(c)
        half = pieces[c][4] // 2
        cols = pl.ds(pieces[c][3] + (0 if d == 1 else half), half)
        slab = gathered.at[k, row, (column + RING - d) % RING, rows, cols]
        return remote(
            slab, slab, row_send.at[c, d - 1], row_recv.at[c, d - 1], beside[d - 1]
        )

    def col_copy(c, d):
        k, rows, cols = place(c)
        slab = gathered.at[k, row, (column + RING - d) % RING, rows, cols]
        return remote(slab, slab, col_send.at[c, d], col_recv.at[c, d], across)

    def turn_copy(c, d):
        k, rows, cols = place(c)
        slab = gathered.at[k, other, column, rows, cols]
        return remote(slab, slab, col_send.at[c, d], col_recv.at[c, d], beside[d - 1])

    def shape(c):
        return pieces[c][2], pieces[c][4]

    def weighted(c, r):
        k, rows, cols = place(c)
        start = base[k, r, rows, cols].astype(jnp.float32)
        total = tiled(count[0], shape(c)) * (start - own[k, r, rows, cols].astype(jnp.float32))
        for d in range(1, RING):
            total = total + tiled(count[d], shape(c)) * (
                start - got[d - 1, k, r, rows, cols].astype(jnp.float32)
            )
        return start, total

    def send_terms(c):
        for d in range(1, RING):
            term_copy(c, d).start()

    def send_part(c):
        for d in range(1, RING):
            term_copy(c, d).wait_recv()
        k, rows, cols = place(c)
        part_sent[k, rows, cols] = weighted(c, other)[1]
        part_copy(c).start()
        held[k, rows, cols] = weighted(c, row)[1]

    def update(c):
        part_copy(c).wait_recv()
        k, rows, cols = place(c)
        start = base[k, row, rows, cols].astype(jnp.float32)
        pseudo = (held[k, rows, cols] + part_got[k, rows, cols]) * tiled(count[RING + 2], shape(c))
        next_moment = momentum_rate * moment[k, rows, cols] + pseudo
        next_weights = start - outer_rate * (pseudo + momentum_rate * next_moment)
        gathered[k, row, column, rows, cols] = next_weights.astype(gathered.dtype)
        moment_next[k, rows, cols] = next_moment
        col_copy(c, 0).start()
        for d in NEXT:
            row_copy(c, d).start()

    def relay(c):
        for d in NEXT:
            row_copy(c, d).wait_recv()
            relay_copy(c, d).start()
            if d not in along_x(c):
                col_copy(c, d).start()

    def forward(c):
        for d in NEXT:
            relay_copy(c, d).wait_recv()
        col_copy(c, 2).start()

    def turn(c):
        col_copy(c, 0).wait_recv()
        for d in along_x(c):
            turn_copy(c, d).start()

    def finish(c):
        for d in range(1, RING):
            col_copy(c, d).wait_recv()

    for d in range(1, RING):
        count_copy(d).start()
    steps = schedule(pieces)
    first = steps.index(("p", 0))
    for stage, c in steps[:first]:
        send_terms(c)
    for d in range(1, RING):
        count_copy(d).wait_recv()
    count[RING] = count[0] + count[1] + count[2] + count[3]
    row_count_copy().start()
    for load in loads:
        load.wait()

    run = {"r": relay, "s": send_terms, "p": send_part, "u": update, "f": forward, "x": turn, "e": finish}
    for stage, c in steps[first:]:
        if stage == "u" and c == 0:
            row_count_copy().wait_recv()
            count[RING + 2] = 1.0 / (count[RING] + count[RING + 1])
        run[stage](c)

    for d in range(1, RING):
        count_copy(d).wait_send()
    row_count_copy().wait_send()
    for c in range(chunks):
        for d in range(1, RING):
            term_copy(c, d).wait_send()
        for d in NEXT:
            row_copy(c, d).wait_send()
            relay_copy(c, d).wait_send()
        part_copy(c).wait_send()
        for d in range(RING):
            col_copy(c, d).wait_send()


def store_kernel(weights, moments, weights_out, moments_out, sem):
    copies = [
        pltpu.make_async_copy(weights, weights_out, sem.at[0]),
        pltpu.make_async_copy(moments, moments_out, sem.at[1]),
    ]
    for copy in copies:
        copy.start()
    for copy in copies:
        copy.wait()


def store(weights, moments):
    anywhere = pl.BlockSpec(memory_space=pl.ANY)
    return pl.pallas_call(
        store_kernel,
        out_shape=(
            jax.ShapeDtypeStruct(weights.shape, weights.dtype),
            jax.ShapeDtypeStruct(moments.shape, moments.dtype),
        ),
        in_specs=[anywhere, anywhere],
        out_specs=(anywhere, anywhere),
        scratch_shapes=[pltpu.SemaphoreType.DMA((2,))],
        compiler_params=pltpu.CompilerParams(vmem_limit_bytes=4 << 20),
        name="store",
    )(weights, moments)


def on_device(counts, inner, anchor, momentum):
    layers, kinds, owned, width = momentum.shape
    blocks = layers * kinds
    chunks = len(chunk_list(owned, width))
    split = (blocks, ROWS, RING, owned, width)
    dma = pltpu.SemaphoreType.DMA
    anywhere = pl.BlockSpec(memory_space=pltpu.HBM)
    weights, moments = pl.pallas_call(
        functools.partial(kernel, blocks, owned, width),
        out_shape=(
            jax.ShapeDtypeStruct(split, anchor.dtype),
            jax.ShapeDtypeStruct((blocks, owned, width), momentum.dtype),
        ),
        in_specs=[pl.BlockSpec(memory_space=pltpu.SMEM), anywhere, anywhere, anywhere],
        out_specs=(pl.BlockSpec(memory_space=pltpu.VMEM),) * 2,
        scratch_shapes=[
            pltpu.VMEM((blocks, ROWS, owned, width), inner.dtype),
            pltpu.VMEM((blocks, ROWS, owned, width), anchor.dtype),
            pltpu.VMEM((blocks, owned, width), jnp.float32),
            pltpu.VMEM((RING - 1, blocks, ROWS, owned, width), inner.dtype),
            pltpu.VMEM((RING + 3, 8, 128), jnp.float32),
            pltpu.VMEM((blocks, owned, width), jnp.float32),
            pltpu.VMEM((blocks, owned, width), jnp.float32),
            pltpu.VMEM((blocks, owned, width), jnp.float32),
            dma((3,)),
            dma((RING,)),
            dma((RING,)),
            dma((chunks, RING - 1)),
            dma((chunks, RING - 1)),
            dma((chunks,)),
            dma((chunks,)),
            dma((chunks, RING)),
            dma((chunks, RING)),
            dma((chunks, RING)),
            dma((chunks, RING)),
        ],
        compiler_params=pltpu.CompilerParams(
            collective_id=0, has_side_effects=True, vmem_limit_bytes=40 << 20
        ),
        name="outer_step",
    )(
        counts,
        pltpu.with_memory_space_constraint(inner.reshape(split), pltpu.HBM),
        pltpu.with_memory_space_constraint(anchor.reshape(split), pltpu.HBM),
        pltpu.with_memory_space_constraint(momentum.reshape(blocks, owned, width), pltpu.HBM),
    )
    weights, moments = store(weights, moments)
    return weights.reshape(anchor.shape), moments.reshape(momentum.shape)


def solution(mesh):
    placed = (
        P("replica"),
        P("replica", None, None, "fsdp", None),
        P(None, None, "fsdp", None),
        P(None, None, ("fsdp", "replica"), None),
    )
    return jax.shard_map(
        on_device,
        mesh=mesh,
        in_specs=placed,
        out_specs=(P(None, None, "fsdp", None), P(None, None, ("fsdp", "replica"), None)),
        check_vma=False,
    )
```

```python
import functools

import jax
import jax.numpy as jnp
from jax import lax
from jax.experimental import pallas as pl
from jax.experimental.pallas import tpu as pltpu
from jax.sharding import PartitionSpec as P

MESH = pl.DeviceIdType.MESH

outer_rate = 0.7
momentum_rate = 0.9

RING = 4
ROWS = 2
SIZES = (16,) * 12
AHEAD = 32.0
UPDATE_LAG = 24.0
RELAY_LAG = 56.0
TURN_LAG = 72.0
FORWARD_LAG = 88.0
FINISH_LAG = 1000.0
ORDER = "purxfs"
LATE = 96
TURNED = (1, 3)
NEXT = (1, 3)


def chunk_list(owned, width):
    chunks, done = [], 0
    for rows in SIZES:
        k, row = divmod(done, owned)
        chunks.append((k, row, rows, 0, width, done, done + rows))
        done += rows
    return chunks


def schedule(chunks):
    steps = []
    for c, (*_, before, after) in enumerate(chunks):
        steps += [
            (max(before - AHEAD, 0.0), ORDER.index("s"), c, "s"),
            (after, ORDER.index("p"), c, "p"),
            (after + UPDATE_LAG, ORDER.index("u"), c, "u"),
            (after + FORWARD_LAG, ORDER.index("f"), c, "f"),
            (after + RELAY_LAG, ORDER.index("r"), c, "r"),
            (after + TURN_LAG, ORDER.index("x"), c, "x"),
            (after + FINISH_LAG, len(ORDER), c, "e"),
        ]
    return [(stage, c) for _, _, c, stage in sorted(steps)]


def tiled(tile, shape):
    wide = jnp.concatenate([tile] * (shape[1] // tile.shape[1]), axis=1)
    return jnp.concatenate([wide] * (shape[0] // tile.shape[0]), axis=0)


def kernel(
    blocks, owned, width,
    counts, inner, anchor, momentum,
    gathered, moment_next,
    own, base, moment, got, count, part_sent, part_got, held,
    load_sem, count_send, count_recv,
    term_send, term_recv, part_send, part_recv, row_send, row_recv, col_send, col_recv,
):
    me = lax.axis_index("replica")
    row, column = me // RING, me % RING
    other = 1 - row
    across = other * RING + column
    beside = [row * RING + (column + d) % RING for d in range(1, RING)]
    pieces = chunk_list(owned, width)
    chunks = len(pieces)

    def place(c):
        k, row, rows, col, cols, _, _ = pieces[c]
        return k, pl.ds(row, rows), pl.ds(col, cols)

    def along_x(c):
        return TURNED if pieces[c][5] >= blocks * owned - LATE else ()

    def remote(src, dst, send, recv, device):
        return pltpu.make_async_remote_copy(
            src_ref=src,
            dst_ref=dst,
            send_sem=send,
            recv_sem=recv,
            device_id={"replica": device},
            device_id_type=MESH,
        )

    barrier = pltpu.get_barrier_semaphore()
    for device in [*beside, across]:
        pl.semaphore_signal(
            barrier, inc=1, device_id={"replica": device}, device_id_type=MESH
        )
    loads = [
        pltpu.make_async_copy(inner.at[:, :, column], own, load_sem.at[0]),
        pltpu.make_async_copy(anchor.at[:, :, column], base, load_sem.at[1]),
        pltpu.make_async_copy(momentum, moment, load_sem.at[2]),
    ]
    for load in loads:
        load.start()
    count[0] = jnp.full(count.shape[1:], counts[0].astype(jnp.float32))

    pl.semaphore_wait(barrier, RING)

    def count_copy(d):
        return remote(
            count.at[0], count.at[d], count_send.at[d], count_recv.at[d], beside[d - 1]
        )

    def row_count_copy():
        return remote(
            count.at[RING], count.at[RING + 1], count_send.at[0], count_recv.at[0], across
        )

    def term_copy(c, d):
        k, rows, cols = place(c)
        return remote(
            inner.at[k, :, (column + d) % RING, rows, cols],
            got.at[d - 1, k, :, rows, cols],
            term_send.at[c, d - 1],
            term_recv.at[c, d - 1],
            beside[d - 1],
        )

    def part_copy(c):
        k, rows, cols = place(c)
        return remote(
            part_sent.at[k, rows, cols],
            part_got.at[k, rows, cols],
            part_send.at[c],
            part_recv.at[c],
            across,
        )

    def row_copy(c, d):
        k, rows, cols = place(c)
        mine = gathered.at[k, row, column, rows, cols]
        return remote(mine, mine, row_send.at[c, d], row_recv.at[c, d], beside[d - 1])

    def relay_copy(c, d):
        k, rows, _ = place(c)
        half = pieces[c][4] // 2
        cols = pl.ds(pieces[c][3] + (0 if d == 1 else half), half)
        slab = gathered.at[k, row, (column + RING - d) % RING, rows, cols]
        return remote(
            slab, slab, row_send.at[c, d - 1], row_recv.at[c, d - 1], beside[d - 1]
        )

    def col_copy(c, d):
        k, rows, cols = place(c)
        slab = gathered.at[k, row, (column + RING - d) % RING, rows, cols]
        return remote(slab, slab, col_send.at[c, d], col_recv.at[c, d], across)

    def turn_copy(c, d):
        k, rows, cols = place(c)
        slab = gathered.at[k, other, column, rows, cols]
        return remote(slab, slab, col_send.at[c, d], col_recv.at[c, d], beside[d - 1])

    def shape(c):
        return pieces[c][2], pieces[c][4]

    def weighted(c, r):
        k, rows, cols = place(c)
        start = base[k, r, rows, cols].astype(jnp.float32)
        total = tiled(count[0], shape(c)) * (start - own[k, r, rows, cols].astype(jnp.float32))
        for d in range(1, RING):
            total = total + tiled(count[d], shape(c)) * (
                start - got[d - 1, k, r, rows, cols].astype(jnp.float32)
            )
        return start, total

    def send_terms(c):
        for d in range(1, RING):
            term_copy(c, d).start()

    def send_part(c):
        for d in range(1, RING):
            term_copy(c, d).wait_recv()
        k, rows, cols = place(c)
        part_sent[k, rows, cols] = weighted(c, other)[1]
        part_copy(c).start()
        held[k, rows, cols] = weighted(c, row)[1]

    def update(c):
        part_copy(c).wait_recv()
        k, rows, cols = place(c)
        start = base[k, row, rows, cols].astype(jnp.float32)
        pseudo = (held[k, rows, cols] + part_got[k, rows, cols]) * tiled(count[RING + 2], shape(c))
        next_moment = momentum_rate * moment[k, rows, cols] + pseudo
        next_weights = start - outer_rate * (pseudo + momentum_rate * next_moment)
        gathered[k, row, column, rows, cols] = next_weights.astype(gathered.dtype)
        moment_next[k, rows, cols] = next_moment
        col_copy(c, 0).start()
        for d in NEXT:
            row_copy(c, d).start()

    def relay(c):
        for d in NEXT:
            row_copy(c, d).wait_recv()
            relay_copy(c, d).start()
            if d not in along_x(c):
                col_copy(c, d).start()

    def forward(c):
        for d in NEXT:
            relay_copy(c, d).wait_recv()
        col_copy(c, 2).start()

    def turn(c):
        col_copy(c, 0).wait_recv()
        for d in along_x(c):
            turn_copy(c, d).start()

    def finish(c):
        for d in range(1, RING):
            col_copy(c, d).wait_recv()

    for d in range(1, RING):
        count_copy(d).start()
    steps = schedule(pieces)
    first = steps.index(("p", 0))
    for stage, c in steps[:first]:
        send_terms(c)
    for d in range(1, RING):
        count_copy(d).wait_recv()
    count[RING] = count[0] + count[1] + count[2] + count[3]
    row_count_copy().start()
    for load in loads:
        load.wait()

    run = {"r": relay, "s": send_terms, "p": send_part, "u": update, "f": forward, "x": turn, "e": finish}
    for stage, c in steps[first:]:
        if stage == "u" and c == 0:
            row_count_copy().wait_recv()
            count[RING + 2] = 1.0 / (count[RING] + count[RING + 1])
        run[stage](c)

    for d in range(1, RING):
        count_copy(d).wait_send()
    row_count_copy().wait_send()
    for c in range(chunks):
        for d in range(1, RING):
            term_copy(c, d).wait_send()
        for d in NEXT:
            row_copy(c, d).wait_send()
            relay_copy(c, d).wait_send()
        part_copy(c).wait_send()
        for d in range(RING):
            col_copy(c, d).wait_send()


def store_kernel(weights, moments, weights_out, moments_out, sem):
    copies = [pltpu.make_async_copy(moments, moments_out, sem.at[0])]
    for k in range(weights.shape[0]):
        copies.append(
            pltpu.make_async_copy(weights.at[k], weights_out.at[k], sem.at[k + 1])
        )
    for copy in copies:
        copy.start()
    for copy in copies:
        copy.wait()


def store(weights, moments):
    anywhere = pl.BlockSpec(memory_space=pl.ANY)
    return pl.pallas_call(
        store_kernel,
        out_shape=(
            jax.ShapeDtypeStruct(weights.shape, weights.dtype),
            jax.ShapeDtypeStruct(moments.shape, moments.dtype),
        ),
        in_specs=[anywhere, anywhere],
        out_specs=(anywhere, anywhere),
        scratch_shapes=[pltpu.SemaphoreType.DMA((weights.shape[0] + 1,))],
        compiler_params=pltpu.CompilerParams(vmem_limit_bytes=4 << 20),
        name="store",
    )(weights, moments)


def on_device(counts, inner, anchor, momentum):
    layers, kinds, owned, width = momentum.shape
    blocks = layers * kinds
    chunks = len(chunk_list(owned, width))
    split = (blocks, ROWS, RING, owned, width)
    dma = pltpu.SemaphoreType.DMA
    anywhere = pl.BlockSpec(memory_space=pltpu.HBM)
    weights, moments = pl.pallas_call(
        functools.partial(kernel, blocks, owned, width),
        out_shape=(
            jax.ShapeDtypeStruct(split, anchor.dtype),
            jax.ShapeDtypeStruct((blocks, owned, width), momentum.dtype),
        ),
        in_specs=[pl.BlockSpec(memory_space=pltpu.SMEM), anywhere, anywhere, anywhere],
        out_specs=(pl.BlockSpec(memory_space=pltpu.VMEM),) * 2,
        scratch_shapes=[
            pltpu.VMEM((blocks, ROWS, owned, width), inner.dtype),
            pltpu.VMEM((blocks, ROWS, owned, width), anchor.dtype),
            pltpu.VMEM((blocks, owned, width), jnp.float32),
            pltpu.VMEM((RING - 1, blocks, ROWS, owned, width), inner.dtype),
            pltpu.VMEM((RING + 3, 8, 128), jnp.float32),
            pltpu.VMEM((blocks, owned, width), jnp.float32),
            pltpu.VMEM((blocks, owned, width), jnp.float32),
            pltpu.VMEM((blocks, owned, width), jnp.float32),
            dma((3,)),
            dma((RING,)),
            dma((RING,)),
            dma((chunks, RING - 1)),
            dma((chunks, RING - 1)),
            dma((chunks,)),
            dma((chunks,)),
            dma((chunks, RING)),
            dma((chunks, RING)),
            dma((chunks, RING)),
            dma((chunks, RING)),
        ],
        compiler_params=pltpu.CompilerParams(
            collective_id=0, has_side_effects=True, vmem_limit_bytes=40 << 20
        ),
        name="outer_step",
    )(
        counts,
        pltpu.with_memory_space_constraint(inner.reshape(split), pltpu.HBM),
        pltpu.with_memory_space_constraint(anchor.reshape(split), pltpu.HBM),
        pltpu.with_memory_space_constraint(momentum.reshape(blocks, owned, width), pltpu.HBM),
    )
    weights, moments = store(weights, moments)
    return weights.reshape(anchor.shape), moments.reshape(momentum.shape)


def solution(mesh):
    placed = (
        P("replica"),
        P("replica", None, None, "fsdp", None),
        P(None, None, "fsdp", None),
        P(None, None, ("fsdp", "replica"), None),
    )
    return jax.shard_map(
        on_device,
        mesh=mesh,
        in_specs=placed,
        out_specs=(P(None, None, "fsdp", None), P(None, None, ("fsdp", "replica"), None)),
        check_vma=False,
    )
```
